32 devices in a mesh: ctx: 16 (over z, x, core), exp: 2 (over y).
Axes of the slice: x: 2, y: 2, z: 4, core: 2. Of those that a mesh axis runs over, the one named last changes fastest.
Arguments:
- feature_in: bfloat16 [6144, 4096], P('ctx', 'exp'), may hold values from -6 to 6
- grad_out: bfloat16 [6144, 4096], P('ctx', 'exp'), may hold values from -6 to 6
- delta: float32 [64, 6144], P('exp', 'ctx'), may hold values from 0.5 to 2
- decay_log: float32 [64], P('exp'), may hold values from -13 to -2
- skip_gain: float32 [64], P('exp'), may hold values from 0.5 to 1.5
- b_proj: float32 [6144, 128], P('ctx'), may hold values from -0.0625 to 0.0625
- c_proj: float32 [6144, 128], P('ctx'), may hold values from -6 to 6
- route_ids: int32 [6144, 4], P('ctx'), may hold values from 0 to 7, all different within a row; in each aligned block of 384 rows (0 to 383, 384 to 767, ...) at most 240 rows name the same one
- route_probs: float32 [6144, 4], P('ctx'), may hold values from 0.05 to 0.5
- w_down: bfloat16 [8, 384, 4096], P('exp'), may hold values from -0.3125 to 0.3125
- saved_act: bfloat16 [16, 8, 240, 384], P('ctx', 'exp'), may hold values from -0.75 to 0.75
Outputs:
- grad_x: bfloat16 [6144, 4096], P('ctx', 'exp')
- grad_delta: float32 [64, 6144], P('exp', 'ctx')
- grad_b: float32 [6144, 128], P(('ctx', 'exp'))
- grad_c: float32 [6144, 128], P(('ctx', 'exp'))
- grad_act: bfloat16 [16, 8, 240, 384], P('ctx', 'exp')
- grad_slots: float32 [16, 8, 240], P('ctx', 'exp')
The draws below stay inside these ranges and needn't reach their ends.
Inputs may be any that keep to these rules, and one draw needn't show every extreme that they name: `route_ids`: each row names 4 different experts; among the rows of one context shard no expert is named more than 240 times, a bound that some block reaches.
All inputs are finite; a program needn't handle non-finite values.
Results may differ from the reference program's by a relative error of at most 0.0049.
Values may be sent and summed in bfloat16 or wider, within the bound.
A program may use at most 256 MiB of HBM per device.

```python
import math
from functools import partial
import jax
import jax.numpy as jnp
import numpy as np
from jax import lax

HEADS = 64
HEAD_DIM = 64
NSTATE = 128
D = 4096
FF = 384
EXPERTS = 8
TOPK = 4
GROUP = 128
SEQ_DEV = 384
SEQ = 6144
CAP = 240
N_CTX = 16


def draw_decay_log(key, part):
    key_pick, key_slow, key_fast = jax.random.split(jax.random.fold_in(key, 11), 3)
    slow_share = 0.5
    chosen = jax.random.uniform(key_pick, (HEADS,), jnp.float32) < slow_share
    slow_rate = jax.random.uniform(key_slow, (HEADS,), jnp.float32, math.log(0.2 / SEQ), math.log(1.5 / SEQ))
    fast_rate = jax.random.uniform(key_fast, (HEADS,), jnp.float32, math.log(1.0 / 60.0), math.log(1.0 / 20.0))
    return jnp.where(chosen, slow_rate, fast_rate).astype(jnp.float32)


def block_levels(stream_key, dims, shards, low, largest):
    def one(dim, shards_of):
        heights = jax.random.uniform(jax.random.fold_in(jax.random.fold_in(stream_key, 6), dim), (shards_of,), jnp.float32, low / len(shards), largest / len(shards))
        return jnp.repeat(jnp.exp(heights), dims[dim] // shards_of).reshape((-1,) + (1,) * (len(dims) - dim - 1))

    level = one(*shards[0])
    for cut in shards[1:]:
        level = level * one(*cut)
    return level


def routed_block(stream_key, own, number, rows, number_of, top, bound, slope):
    sequence = jax.random.permutation(stream_key, number_of)
    crowded, usual = load_shares(number_of, rows * top, bound, slope, True), load_shares(number_of, rows * top, bound, slope, False)
    places = jnp.arange(number_of)

    def named(lengths, rotation):
        used = int((lengths > 0).sum())
        fixed = max(1, used // 4)
        shifted = fixed + (places - fixed + rotation * (used - fixed)) % max(1, number_of - fixed)
        return jnp.zeros((number_of,), jnp.int32).at[sequence[jnp.where(places < fixed, places, shifted)]].set(jnp.asarray(lengths, jnp.int32))

    lengths = jnp.where(number % 4 == 0, named(crowded, number // 4), named(usual, number - number // 4 - 1))
    mixed = jax.random.permutation(jax.random.fold_in(own, 3), number_of)
    giver, taker = mixed[0:number_of // 2 * 2:2], mixed[1:number_of // 2 * 2:2]
    margin = jnp.minimum(lengths[giver] - 1, bound - lengths[taker]) // 2
    margin = jnp.where((giver == sequence[0]) | (taker == sequence[0]) | (lengths[taker] == 0), 0, jnp.maximum(margin, 0))
    shifted = jax.random.randint(jax.random.fold_in(own, 4), (number_of // 2,), 0, 1 << 20) % (margin + 1)
    lengths = lengths.at[giver].add(-shifted).at[taker].add(shifted)
    items = jnp.searchsorted(jnp.cumsum(lengths), jnp.arange(rows * top), side="right").astype(jnp.int32)
    table = items.reshape(top, rows).T
    table = table[jax.random.permutation(jax.random.fold_in(own, 1), rows)]
    rotation = jax.random.randint(jax.random.fold_in(own, 2), (rows, 1), 0, top)
    return jnp.take_along_axis(table, (jnp.arange(top)[None, :] + rotation) % top, axis=1)


def load_shares(count, total, reach, skew, full):
    portions = [(1 << 20) // math.isqrt(rank ** skew) + 1 for rank in range(1, count + 1)]
    largest = reach if full else min(reach, max(-(-total // count), total * portions[0] // sum(portions)))
    least = 1 if total - largest >= count - 1 else 0
    holding, rest = [largest] + [least] * (count - 1), total - largest - least * (count - 1)
    while rest > 0:
        free = [i for i in range(1, count) if holding[i] < largest] or [i for i in range(1, count) if holding[i] < reach]
        mass, budget = sum([portions[i] for i in free]), rest
        for i in free:
            extra = min(reach - holding[i], max(1, budget * portions[i] // mass), rest)
            holding[i] = holding[i] + extra
            rest = rest - extra
    return np.array(holding)


def gaussian(stream_key, dims, scale, bound, cuts=(), held_as=jnp.bfloat16):
    entries = jax.random.normal(stream_key, dims, jnp.float32) * scale
    if len(cuts) > 0:
        entries = block_levels(stream_key, dims, cuts, -0.22, 0.18) * entries
    return jnp.clip(entries, min=-bound, max=bound).astype(held_as)


def setup_inputs(seed: int = 0) -> dict:
    key_list = jax.random.split(jax.random.key(seed), 12)
    feature_in = gaussian(key_list[0], (SEQ, D), 1.0, 6.0, ((0, 16), (1, 2)))
    grad_out = gaussian(key_list[1], (SEQ, D), 1.0, 6.0, ((0, 16), (1, 2)))
    delta = jnp.clip(0.5 + 1.5 * jax.random.uniform(key_list[2], (HEADS, SEQ), jnp.float32) ** block_levels(key_list[2], (HEADS, SEQ), ((0, 2), (1, 16)), -0.2, 0.2), 0.5, 2.0)
    decay_log = draw_decay_log(jax.random.fold_in(key_list[11], 71), 0)
    skip_gain = jnp.clip(0.5 + 1.0 * jax.random.uniform(key_list[4], (HEADS,), jnp.float32) ** block_levels(key_list[4], (HEADS,), ((0, 2),), -0.2, 0.2), 0.5, 1.5)
    b_proj = gaussian(key_list[5], (SEQ, NSTATE), 0.004, 0.0625, ((0, 16),), jnp.float32)
    c_proj = gaussian(key_list[6], (SEQ, NSTATE), 1.0, 6.0, ((0, 16),), jnp.float32)
    route_ids_keys = jax.random.split(jax.random.fold_in(key_list[7], 1), SEQ // SEQ_DEV)
    route_ids_turns = jax.random.permutation(jax.random.fold_in(key_list[7], 3), SEQ // SEQ_DEV)
    route_ids = jax.vmap(lambda own, number: routed_block(jax.random.fold_in(key_list[7], 2), own, number, SEQ_DEV, EXPERTS, TOPK, CAP, 2))(route_ids_keys, route_ids_turns).reshape((SEQ, TOPK))
    route_probs = jnp.clip(0.05 + 0.45 * jax.random.uniform(key_list[8], (SEQ, TOPK), jnp.float32) ** block_levels(key_list[8], (SEQ, TOPK), ((0, 16),), -0.2, 0.2), 0.05, 0.5)
    w_down = gaussian(key_list[9], (EXPERTS, FF, D), FF ** -0.5, 0.3125, ((0, 2),))
    saved_act = gaussian(key_list[10], (N_CTX, EXPERTS, CAP, FF), 0.05, 0.75, ((0, 16), (1, 2)))
    return dict(feature_in=feature_in, grad_out=grad_out, delta=delta, decay_log=decay_log, skip_gain=skip_gain, b_proj=b_proj, c_proj=c_proj, route_ids=route_ids, route_probs=route_probs, w_down=w_down, saved_act=saved_act)


HIGHEST = lax.Precision.HIGHEST

def block_step(neg_rate, skip_gain, carry_state, pieces):
    inputs, deltas, b_block, c_block = pieces
    block_len = inputs.shape[0]
    logdecay = jnp.cumsum(neg_rate[:, None] * deltas, axis=1)
    gram_mat = jnp.dot(c_block, b_block.T, precision=HIGHEST)
    causal = jnp.arange(block_len, dtype=jnp.int32)[:, None] >= jnp.arange(block_len, dtype=jnp.int32)[None, :]
    spread = logdecay[:, :, None] - logdecay[:, None, :]
    weights = jnp.exp(jnp.where(causal[None], spread, -jnp.inf))
    driven = inputs * deltas.T[:, :, None]
    within = jnp.einsum('hts,ts,shp->thp', weights, gram_mat, driven, precision=HIGHEST)
    carried = jnp.einsum('tn,hpn->thp', c_block, carry_state, precision=HIGHEST) * jnp.exp(logdecay).T[:, :, None]
    outputs = within + carried + skip_gain[None, :, None] * inputs
    remain = jnp.exp(logdecay[:, -1:] - logdecay)
    updated = jnp.exp(logdecay[:, -1])[:, None, None] * carry_state + jnp.einsum('sn,shp,hs->hpn', b_block, driven, remain, precision=HIGHEST)
    return (updated, outputs)

def run_blocks(inputs, deltas, b_full, c_full, start_state, neg_rate, skip_gain, block_len, recompute):
    length, head_count, width = inputs.shape
    block_count = length // block_len
    x_blocks = inputs.reshape(block_count, block_len, head_count, width)
    d_blocks = deltas.reshape(head_count, block_count, block_len).transpose(1, 0, 2)
    b_blocks = b_full.reshape(block_count, block_len, -1)
    c_blocks = c_full.reshape(block_count, block_len, -1)
    block_fn = partial(block_step, neg_rate, skip_gain)
    if recompute:
        block_fn = jax.checkpoint(block_fn)
    final_state, outputs = lax.scan(block_fn, start_state, (x_blocks, d_blocks, b_blocks, c_blocks))
    return (outputs.reshape(length, head_count, width), final_state)

def slot_tables(route_ids, route_probs, expert_count, capacity):
    row_count, top_count = route_ids.shape
    flat_ids = route_ids.reshape(-1).astype(jnp.int32)
    one_hot = (flat_ids[:, None] == jnp.arange(expert_count, dtype=jnp.int32)[None, :]).astype(jnp.int32)
    before = jnp.cumsum(one_hot, axis=0).astype(jnp.int32) - one_hot
    slot_rank = lax.optimization_barrier(jnp.sum(before * one_hot, axis=1)).astype(jnp.int32)
    position = (flat_ids * capacity + slot_rank).astype(jnp.int32)
    token_row = (jnp.arange(row_count * top_count, dtype=jnp.int32) // top_count).astype(jnp.int32)
    slot_table = jnp.full((expert_count * capacity,), row_count, dtype=jnp.int32).at[position].set(token_row)
    weight = jnp.zeros((expert_count * capacity,), jnp.float32).at[position].set(route_probs.reshape(-1))
    return (slot_table.reshape(expert_count, capacity), weight.reshape(expert_count, capacity))

def expert_grad(picked, weights_down, act_rows, slot_probs):
    out_row = jnp.dot(act_rows, weights_down, preferred_element_type=jnp.float32)
    grad_slot = lax.optimization_barrier(jnp.sum(picked.astype(jnp.float32) * out_row, axis=1))
    scaled = (slot_probs[:, None] * picked.astype(jnp.float32)).astype(jnp.bfloat16)
    grad_rows = jnp.dot(scaled, weights_down.T, preferred_element_type=jnp.float32).astype(jnp.bfloat16)
    return (grad_rows, grad_slot)

def reference(feature_in, grad_out, delta, decay_log, skip_gain, b_proj, c_proj, route_ids, route_probs, w_down, saved_act):
    neg_rate = -jnp.exp(decay_log)
    inputs = feature_in.astype(jnp.float32).reshape(SEQ, HEADS, HEAD_DIM)
    cotangent = grad_out.astype(jnp.float32).reshape(SEQ, HEADS, HEAD_DIM)
    zero_state = jnp.zeros((HEADS, HEAD_DIM, NSTATE), jnp.float32)

    def forward(feats, deltas, b_full, c_full):
        return run_blocks(feats, deltas, b_full, c_full, zero_state, neg_rate, skip_gain, GROUP, True)[0]
    _, pullback = jax.vjp(forward, inputs, delta, b_proj.astype(jnp.float32), c_proj.astype(jnp.float32))
    grad_feat, grad_delta, grad_b, grad_c = pullback(cotangent)
    grad_rows_all = grad_out.reshape(N_CTX, SEQ_DEV, D)
    ids_all = route_ids.reshape(N_CTX, SEQ_DEV, TOPK)
    probs_all = route_probs.reshape(N_CTX, SEQ_DEV, TOPK)

    def one_shard(pieces):
        shard_rows, shard_ids, shard_probs, shard_acts = pieces
        slot_table, slot_probs = slot_tables(shard_ids, shard_probs, EXPERTS, CAP)
        padded = jnp.concatenate([shard_rows, jnp.zeros((1, D), shard_rows.dtype)], axis=0)

        def one_expert(items):
            index_rows, weights_down, act_rows, probs_slot = items
            return expert_grad(padded[index_rows], weights_down, act_rows, probs_slot)
        return lax.map(one_expert, (slot_table, w_down, shard_acts, slot_probs))
    grad_act, grad_slots = lax.map(one_shard, (grad_rows_all, ids_all, probs_all, saved_act))
    return (grad_feat.reshape(SEQ, D).astype(jnp.bfloat16), grad_delta, grad_b, grad_c, grad_act, grad_slots)
```

```python
from functools import partial

import jax
import jax.numpy as jnp
from jax import lax
from jax.experimental import pallas as pl
from jax.experimental.pallas import tpu as pltpu
from jax.sharding import PartitionSpec as P

HEAD_DIM = 64
CHUNK = 128
LANES = 128
HIGHEST = lax.Precision.HIGHEST
F32 = jnp.float32
BF16 = jnp.bfloat16
MESH = pl.DeviceIdType.MESH


def nn(a, b, precision=None):
    return lax.dot_general(
        a, b, (((1,), (0,)), ((), ())), precision=precision, preferred_element_type=F32
    )


def nt(a, b, precision=None):
    return lax.dot_general(
        a, b, (((1,), (1,)), ((), ())), precision=precision, preferred_element_type=F32
    )


def split(value, count):
    parts = []
    for _ in range(count):
        part = value.astype(BF16)
        parts.append(part)
        value = value - part.astype(F32)
    return parts


def spread_out(parts, chosen):
    total = nn(parts[0], chosen)
    for part in parts[1:]:
        total = total + nn(part, chosen)
    return total


def iota(shape, dim):
    return lax.broadcasted_iota(jnp.int32, shape, dim)


def head_lanes(heads, width, first):
    return (iota((heads, width), 0) == first + iota((heads, width), 1) // HEAD_DIM).astype(BF16)


def chain_kernel(
    n_ctx, n_exp, pieces,
    x_ref, g_ref, g_any, delta_t_ref, rate_ref, b_t_ref, c_t_ref,
    g_full, enter_ref, leave_ref,
    own_f, own_b, in_f, in_b, out_f, out_b, through_ref,
    send_f, recv_f, send_b, recv_b, send_g, recv_g, local_sem,
):
    me, side = lax.axis_index("ctx"), lax.axis_index("exp")
    right, left = lax.rem(me + 1, n_ctx), lax.rem(me + n_ctx - 1, n_ctx)
    barrier = pltpu.get_barrier_semaphore()
    for other in (left, right):
        pl.semaphore_signal(barrier, inc=1, device_id=(other, side), device_id_type=MESH)
    for k in range(1, n_exp):
        pl.semaphore_signal(
            barrier, inc=1, device_id=(me, lax.rem(side + k, n_exp)), device_id_type=MESH
        )
    pl.semaphore_wait(barrier, 2 + n_exp - 1)

    def to_partner(k):
        return pltpu.make_async_remote_copy(
            src_ref=g_any,
            dst_ref=g_full.at[side],
            send_sem=send_g.at[k - 1],
            recv_sem=recv_g.at[k - 1],
            device_id=(me, lax.rem(side + k, n_exp)),
            device_id_type=MESH,
        )

    for k in range(1, n_exp):
        to_partner(k).start()
    mine = pltpu.make_async_copy(g_any, g_full.at[side], local_sem)
    mine.start()

    length, width = x_ref.shape
    heads = delta_t_ref.shape[1]
    tri = (iota((length, length), 0) >= iota((length, length), 1)).astype(F32)
    delta_t = delta_t_ref[...]
    logdecay = nn(tri, delta_t * rate_ref[...], HIGHEST)
    last = logdecay[length - 1 : length, :]
    grow = split(jnp.exp(logdecay), 3)
    keep = split(jnp.exp(last - logdecay) * delta_t, 2)
    b_t = b_t_ref[...].astype(BF16)
    c_t = c_t_ref[...].astype(BF16)

    @pl.loop(0, width // LANES)
    def _(i):
        lanes = pl.ds(pl.multiple_of(i * LANES, LANES), LANES)
        chosen = head_lanes(heads, LANES, i * (LANES // HEAD_DIM))
        grow_x = spread_out(grow, chosen)
        keep_x = spread_out(keep, chosen)
        own_f[:, lanes] = nn(b_t, (x_ref[:, lanes].astype(F32) * keep_x).astype(BF16))
        own_b[:, lanes] = nn(c_t, (g_ref[:, lanes].astype(F32) * grow_x).astype(BF16))
        through_ref[:, lanes] = jnp.broadcast_to(grow_x[length - 1 : length, :], (8, LANES))

    rows = own_f.shape[0] // pieces

    def hop(source, landing, send, recv, k, target):
        part = pl.ds(pl.multiple_of(k * rows, rows), rows)
        return pltpu.make_async_remote_copy(
            src_ref=source.at[part],
            dst_ref=landing.at[part],
            send_sem=send.at[k],
            recv_sem=recv.at[k],
            device_id=(target, side),
            device_id_type=MESH,
        )

    def handle(k, place, own, landing, outgoing, result, send, recv, target):
        part = pl.ds(pl.multiple_of(k * rows, rows), rows)

        @pl.when(place == 0)
        def _():
            result[part] = jnp.zeros((rows, width), F32)
            outgoing[part] = own[part]

        @pl.when(place > 0)
        def _():
            hop(outgoing, landing, send, recv, k, target).wait_recv()
            arrived = landing[part]
            result[part] = arrived
            outgoing[part] = through_ref[0:1, :] * arrived + own[part]

        @pl.when(place < n_ctx - 1)
        def _():
            hop(outgoing, landing, send, recv, k, target).start()

    back = n_ctx - 1 - me

    def lap(step, carry):
        k_f, k_b = step - me, step - back

        @pl.when((k_f >= 0) & (k_f < pieces))
        def _():
            handle(k_f, me, own_f, in_f, out_f, enter_ref, send_f, recv_f, right)

        @pl.when((k_b >= 0) & (k_b < pieces))
        def _():
            handle(k_b, back, own_b, in_b, out_b, leave_ref, send_b, recv_b, left)

        return carry

    lax.fori_loop(0, n_ctx - 1 + pieces, lap, 0)

    @pl.when(me < n_ctx - 1)
    def _():
        for k in range(pieces):
            hop(out_f, in_f, send_f, recv_f, k, right).wait_send()

    @pl.when(back < n_ctx - 1)
    def _():
        for k in range(pieces):
            hop(out_b, in_b, send_b, recv_b, k, left).wait_send()

    for k in range(1, n_exp):
        to_partner(k).wait_send()
    for k in range(1, n_exp):
        to_partner(k).wait_recv()
    mine.wait()


def scan_kernel(
    x_ref, g_ref, delta_ref, delta_t_ref, rate_row_ref, rate_col_ref, skip_ref,
    b_ref, c_ref, b_t_ref, c_t_ref, enter_ref, leave_ref,
    grad_x_ref, grad_delta_ref, grad_b_ref, grad_c_ref,
    log_row, gram_t, dgram_t, row_u, row_v,
):
    length, width = x_ref.shape
    heads = delta_ref.shape[0]
    chunks = length // CHUNK
    row_id, col_id = iota((length, length), 0), iota((length, length), 1)
    same = row_id // CHUNK == col_id // CHUNK
    lower = ((row_id >= col_id) & same).astype(F32)
    upper = ((row_id <= col_id) & same).astype(F32)
    delta, delta_t = delta_ref[...], delta_t_ref[...]
    log_rows = nn(delta * rate_col_ref[...], upper, HIGHEST)
    for h in range(heads):
        log_row[h] = log_rows[h : h + 1, :]
    log_t = nn(lower, delta_t * rate_row_ref[...], HIGHEST)
    ends = jnp.concatenate(
        [
            jnp.broadcast_to(log_t[(c + 1) * CHUNK - 1 : (c + 1) * CHUNK, :], (CHUNK, heads))
            for c in range(chunks)
        ],
        axis=0,
    )
    grow = split(jnp.exp(log_t), 2)
    keep = split(jnp.exp(ends - log_t) * delta_t, 2)
    offset = split(jnp.log(delta_t) - log_t, 3)
    for c in range(chunks):
        part = slice(c * CHUNK, (c + 1) * CHUNK)
        gram_t[part] = nt(b_ref[part], c_ref[part], HIGHEST)
    dgram_t[...] = jnp.zeros_like(dgram_t)
    row_u[...] = jnp.zeros_like(row_u)
    row_v[...] = jnp.zeros_like(row_v)
    grad_b_ref[...] = jnp.zeros_like(grad_b_ref)
    grad_c_ref[...] = jnp.zeros_like(grad_c_ref)
    causal = iota((CHUNK, CHUNK), 1) >= iota((CHUNK, CHUNK), 0)
    first_half = iota((CHUNK, LANES), 1) < HEAD_DIM
    last_row = iota((CHUNK, LANES), 0) == CHUNK - 1
    head_id = iota((heads, CHUNK), 0)
    per = LANES // HEAD_DIM

    @pl.loop(0, width // LANES)
    def _(i):
        lanes = pl.ds(pl.multiple_of(i * LANES, LANES), LANES)
        chosen = head_lanes(heads, LANES, i * per)
        grow_x = spread_out(grow, chosen)
        keep_x = spread_out(keep, chosen)
        columns = [
            spread_out(offset, (iota((heads, LANES), 0) == i * per + j).astype(BF16))
            for j in range(per)
        ]
        skip = skip_ref[0:1, lanes]
        parts = [slice(c * CHUNK, (c + 1) * CHUNK) for c in range(chunks)]
        xs = [x_ref[part, lanes] for part in parts]
        gs = [g_ref[part, lanes] for part in parts]
        kept = [(xs[c].astype(F32) * keep_x[parts[c]]).astype(BF16) for c in range(chunks)]
        grown = [(gs[c].astype(F32) * grow_x[parts[c]]).astype(BF16) for c in range(chunks)]
        through = [grow_x[(c + 1) * CHUNK - 1 : (c + 1) * CHUNK, :] for c in range(chunks)]
        states = [enter_ref[:, lanes]]
        for c in range(chunks):
            states.append(
                through[c] * states[c] + nn(b_t_ref[:, parts[c]].astype(BF16), kept[c])
            )
        grads = [None] * chunks + [leave_ref[:, lanes]]
        for c in reversed(range(chunks)):
            grads[c] = through[c] * grads[c + 1] + nn(c_t_ref[:, parts[c]].astype(BF16), grown[c])
        for c in range(chunks):
            part = parts[c]
            state, grad = states[c].astype(BF16), grads[c + 1].astype(BF16)
            from_grad = nn(b_ref[part].astype(BF16), grad) * keep_x[part]
            from_state = nn(c_ref[part].astype(BF16), state) * grow_x[part]
            grad_c_ref[part] += nt(grown[c], state)
            grad_b_ref[part] += nt(kept[c], grad)
            gram = gram_t[part]
            total = None
            within = []
            for j in range(per):
                mask = first_half if j == 0 else jnp.logical_not(first_half)
                x_half = jnp.where(mask, xs[c].astype(F32), 0.0).astype(BF16)
                pair = nt(x_half, gs[c])
                log_t_row = log_row[i * per + j, :, part]
                weight = jnp.exp(jnp.where(causal, log_t_row + columns[j][part], -1e30))
                value = weight * pair
                total = value if total is None else total + value
                summed = jnp.sum(value * gram, axis=0, keepdims=True)
                row_u[:, part] += jnp.where(head_id == i * per + j, summed, 0.0)
                within.append(nn((weight * gram).astype(BF16), gs[c]))
            dgram_t[part] += total
            inner = jnp.where(first_half, within[0], within[1]) + from_grad
            g_wide = gs[c].astype(F32)
            grad_x_ref[part, lanes] = (inner + skip * g_wide).astype(BF16)
            used = xs[c].astype(F32) * inner
            ending = jnp.sum(states[c + 1] * grads[c + 1], axis=0, keepdims=True)
            reached = g_wide * from_state + jnp.where(last_row, ending, 0.0)
            for piece in split(used, 2):
                row_v[:, part] += nt(chosen, piece)
            for piece in split(reached, 2):
                row_u[:, part] += nt(chosen, piece)

    drift = nn(row_u[...] - row_v[...], lower, HIGHEST)
    grad_delta_ref[...] = row_v[...] / delta + rate_col_ref[...] * drift
    for c in range(chunks):
        part = slice(c * CHUNK, (c + 1) * CHUNK)
        grad_b_ref[part] += nn(dgram_t[part], c_ref[part], HIGHEST)
        grad_c_ref[part] += nn(dgram_t[part].T, b_ref[part], HIGHEST)


def expert_kernel(
    n_exp,
    g_ref, ids_ref, probs_ref, w_ref, act_ref, b_any, c_any,
    grad_act_ref, grad_slots_ref, out_b, out_c,
    in_b, in_c, send_b, recv_b, send_c, recv_c,
):
    me, side = lax.axis_index("ctx"), lax.axis_index("exp")
    step, steps = pl.program_id(0), pl.num_programs(0)
    rows = out_b.shape[0]

    def hop(k, source, landing, send, recv):
        target = lax.rem(side + k, n_exp)
        return pltpu.make_async_remote_copy(
            src_ref=source.at[pl.ds(pl.multiple_of(target * rows, rows), rows)],
            dst_ref=landing.at[k - 1],
            send_sem=send.at[k - 1],
            recv_sem=recv.at[k - 1],
            device_id=(me, target),
            device_id_type=MESH,
        )

    @pl.when(step == 0)
    def _():
        barrier = pltpu.get_barrier_semaphore()
        for k in range(1, n_exp):
            pl.semaphore_signal(
                barrier, inc=1, device_id=(me, lax.rem(side + k, n_exp)), device_id_type=MESH
            )
        pl.semaphore_wait(barrier, n_exp - 1)
        for k in range(1, n_exp):
            hop(k, b_any, in_b, send_b, recv_b).start()
            hop(k, c_any, in_c, send_c, recv_c).start()

    length = ids_ref.shape[1]
    capacity = act_ref.shape[1]
    part_width = g_ref.shape[2]
    expert = side * steps + step
    named = ids_ref[...] == expert
    hit = jnp.sum(named.astype(F32), axis=0, keepdims=True)
    prob = jnp.sum(jnp.where(named, probs_ref[...], 0.0), axis=0, keepdims=True)
    before = (iota((length, length), 0) < iota((length, length), 1)).astype(BF16)
    rank = nn(jnp.broadcast_to(hit, (16, length)).astype(BF16), before)[0:1, :]
    place = jnp.where(hit > 0.5, rank, -1.0)
    picks = iota((capacity, length), 0).astype(F32) == place
    weight = jnp.sum(jnp.where(picks, prob, 0.0), axis=1, keepdims=True)
    chosen = picks.astype(BF16)
    inner = None
    for j in range(n_exp):
        picked = nn(chosen, g_ref[j]).astype(BF16)
        term = nt(picked, w_ref[0, :, j * part_width : (j + 1) * part_width])
        inner = term if inner is None else inner + term
    grad_act_ref[0] = (weight * inner).astype(BF16)
    product = act_ref[0].astype(F32) * inner
    ones = jnp.ones((16, product.shape[1]), BF16)
    summed = None
    for piece in split(product, 2):
        term = nt(ones, piece)
        summed = term if summed is None else summed + term
    grad_slots_ref[0] = summed[0:1, :]

    @pl.when(step == steps - 1)
    def _():
        mine = pl.ds(pl.multiple_of(side * rows, rows), rows)
        total_b, total_c = b_any[mine], c_any[mine]
        for k in range(1, n_exp):
            hop(k, b_any, in_b, send_b, recv_b).wait()
            hop(k, c_any, in_c, send_c, recv_c).wait()
            total_b = total_b + in_b[k - 1]
            total_c = total_c + in_c[k - 1]
        out_b[...] = total_b
        out_c[...] = total_c


def per_device(
    n_ctx, n_exp,
    feature_in, grad_out, delta, decay_log, skip_gain, b_proj, c_proj,
    route_ids, route_probs, w_down, saved_act,
):
    length, width = feature_in.shape
    heads = delta.shape[0]
    nstate = b_proj.shape[1]
    rate = -jnp.exp(decay_log)
    rate_row, rate_col = rate[None, :], rate[:, None]
    skip = jnp.repeat(skip_gain, HEAD_DIM)[None, :]
    delta_t, b_t, c_t = delta.T, b_proj.T, c_proj.T
    vmem = pl.BlockSpec(memory_space=pltpu.VMEM)
    hbm = pl.BlockSpec(memory_space=pl.ANY)
    state = jax.ShapeDtypeStruct((nstate, width), F32)
    pieces = nstate // 8
    others = n_exp - 1
    g_full, enter, leave = pl.pallas_call(
        partial(chain_kernel, n_ctx, n_exp, pieces),
        out_shape=(jax.ShapeDtypeStruct((n_exp, length, width), BF16), state, state),
        in_specs=[vmem, vmem, hbm, vmem, vmem, vmem, vmem],
        out_specs=(hbm, vmem, vmem),
        scratch_shapes=[pltpu.VMEM((nstate, width), F32)] * 6
        + [pltpu.VMEM((8, width), F32)]
        + [pltpu.SemaphoreType.DMA((pieces,))] * 4
        + [pltpu.SemaphoreType.DMA((others,))] * 2
        + [pltpu.SemaphoreType.DMA],
        compiler_params=pltpu.CompilerParams(
            collective_id=0, has_side_effects=True, vmem_limit_bytes=40 << 20
        ),
        name="state_chain",
    )(feature_in, grad_out, grad_out, delta_t, rate_row, b_t, c_t)

    square = jax.ShapeDtypeStruct((length, nstate), F32)
    grad_x, grad_delta, part_b, part_c = pl.pallas_call(
        scan_kernel,
        out_shape=(
            jax.ShapeDtypeStruct((length, width), BF16),
            jax.ShapeDtypeStruct((heads, length), F32),
            square,
            square,
        ),
        in_specs=[vmem] * 13,
        out_specs=(vmem,) * 4,
        scratch_shapes=[
            pltpu.VMEM((heads, 1, length), F32),
            pltpu.VMEM((length, CHUNK), F32),
            pltpu.VMEM((length, CHUNK), F32),
            pltpu.VMEM((heads, length), F32),
            pltpu.VMEM((heads, length), F32),
        ],
        compiler_params=pltpu.CompilerParams(vmem_limit_bytes=40 << 20),
        name="scan_grads",
    )(
        feature_in, grad_out, delta, delta_t, rate_row, rate_col, skip,
        b_proj, c_proj, b_t, c_t, enter, leave,
    )

    experts, hidden, full = w_down.shape
    capacity = saved_act.shape[2]
    rows = length // n_exp
    whole = lambda *shape: pl.BlockSpec(shape, lambda e: (0,) * len(shape))
    shard = jax.ShapeDtypeStruct((rows, nstate), F32)
    grad_act, grad_slots, grad_b, grad_c = pl.pallas_call(
        partial(expert_kernel, n_exp),
        grid=(experts,),
        out_shape=(
            jax.ShapeDtypeStruct((experts, capacity, hidden), BF16),
            jax.ShapeDtypeStruct((experts, 1, capacity), F32),
            shard,
            shard,
        ),
        in_specs=[
            whole(n_exp, length, width),
            whole(route_ids.shape[1], length),
            whole(route_ids.shape[1], length),
            pl.BlockSpec((1, hidden, full), lambda e: (e, 0, 0)),
            pl.BlockSpec((1, capacity, hidden), lambda e: (e, 0, 0)),
            vmem,
            vmem,
        ],
        out_specs=(
            pl.BlockSpec((1, capacity, hidden), lambda e: (e, 0, 0)),
            pl.BlockSpec((1, 1, capacity), lambda e: (e, 0, 0)),
            whole(rows, nstate),
            whole(rows, nstate),
        ),
        scratch_shapes=[pltpu.VMEM((others, rows, nstate), F32)] * 2
        + [pltpu.SemaphoreType.DMA((others,))] * 4,
        compiler_params=pltpu.CompilerParams(
            collective_id=1, has_side_effects=True, vmem_limit_bytes=40 << 20
        ),
        name="expert_grads",
    )(g_full, route_ids.T, route_probs.T, w_down, saved_act[0], part_b, part_c)
    return (grad_x, grad_delta, grad_b, grad_c, grad_act[None], grad_slots.reshape(1, experts, capacity))


def solution(mesh):
    placed = (
        P("ctx", "exp"),
        P("ctx", "exp"),
        P("exp", "ctx"),
        P("exp"),
        P("exp"),
        P("ctx", None),
        P("ctx", None),
        P("ctx", None),
        P("ctx", None),
        P("exp", None, None),
        P("ctx", "exp", None, None),
    )
    return jax.shard_map(
        partial(per_device, mesh.shape["ctx"], mesh.shape["exp"]),
        mesh=mesh,
        in_specs=placed,
        out_specs=(
            P("ctx", "exp"),
            P("exp", "ctx"),
            P(("ctx", "exp"), None),
            P(("ctx", "exp"), None),
            P("ctx", "exp", None, None),
            P("ctx", "exp", None),
        ),
        check_vma=False,
    )
```

```python
from functools import partial

import jax
import jax.numpy as jnp
from jax import lax
from jax.experimental import pallas as pl
from jax.experimental.pallas import tpu as pltpu
from jax.sharding import PartitionSpec as P

HEAD_DIM = 64
CHUNK = 128
LANES = 128
HIGHEST = lax.Precision.HIGHEST
F32 = jnp.float32
BF16 = jnp.bfloat16
MESH = pl.DeviceIdType.MESH


def nn(a, b, precision=None):
    return lax.dot_general(
        a, b, (((1,), (0,)), ((), ())), precision=precision, preferred_element_type=F32
    )


def nt(a, b, precision=None):
    return lax.dot_general(
        a, b, (((1,), (1,)), ((), ())), precision=precision, preferred_element_type=F32
    )


def split(value, count):
    parts = []
    for _ in range(count):
        part = value.astype(BF16)
        parts.append(part)
        value = value - part.astype(F32)
    return parts


def spread_out(parts, chosen):
    total = nn(parts[0], chosen)
    for part in parts[1:]:
        total = total + nn(part, chosen)
    return total


def iota(shape, dim):
    return lax.broadcasted_iota(jnp.int32, shape, dim)


def head_lanes(heads, width, first):
    return (iota((heads, width), 0) == first + iota((heads, width), 1) // HEAD_DIM).astype(BF16)


def block_kernel(
    n_ctx, n_exp, pieces,
    x_ref, g_ref, delta_ref, delta_t_ref, rate_row_ref, rate_col_ref, skip_ref,
    b_ref, c_ref, b_t_ref, c_t_ref, ids_ref, probs_ref, act_ref, w_any,
    grad_x_ref, grad_delta_ref, grad_b_ref, grad_c_ref, grad_act_ref, grad_slots_ref,
    own_f, own_b, in_f, in_b, out_f, out_b, through_ref, g_in, w_ref,
    log_row, grow_hi, grow_lo, keep_hi, keep_lo, off_hi, off_mid, off_lo,
    gram_t, dgram_t, row_u, row_v, inside, part_b, part_c, land_b, land_c, act_sum,
    send_f, recv_f, send_b, recv_b, send_g, recv_g, load_w, send_p, recv_p, send_q, recv_q,
):
    me, side = lax.axis_index("ctx"), lax.axis_index("exp")
    right, left = lax.rem(me + 1, n_ctx), lax.rem(me + n_ctx - 1, n_ctx)
    barrier = pltpu.get_barrier_semaphore()
    for other in (left, right):
        pl.semaphore_signal(barrier, inc=1, device_id=(other, side), device_id_type=MESH)
    for k in range(1, n_exp):
        pl.semaphore_signal(
            barrier, inc=1, device_id=(me, lax.rem(side + k, n_exp)), device_id_type=MESH
        )
    pl.semaphore_wait(barrier, 2 + n_exp - 1)

    def to_partner(k):
        return pltpu.make_async_remote_copy(
            src_ref=g_ref,
            dst_ref=g_in.at[k - 1],
            send_sem=send_g.at[k - 1],
            recv_sem=recv_g.at[k - 1],
            device_id=(me, lax.rem(side + k, n_exp)),
            device_id_type=MESH,
        )

    for k in range(1, n_exp):
        to_partner(k).start()
    experts = w_ref.shape[0]

    def weights(e):
        return pltpu.make_async_copy(w_any.at[e], w_ref.at[e], load_w.at[e])

    for e in range(experts):
        weights(e).start()

    length, width = x_ref.shape
    heads = delta_t_ref.shape[1]
    chunks = length // CHUNK
    per = LANES // HEAD_DIM
    pairs = width // LANES
    delta, delta_t = delta_ref[...], delta_t_ref[...]
    row_id, col_id = iota((length, length), 0), iota((length, length), 1)
    same = row_id // CHUNK == col_id // CHUNK
    tri = (row_id >= col_id).astype(F32)
    lower = ((row_id >= col_id) & same).astype(F32)
    upper = ((row_id <= col_id) & same).astype(F32)
    pace = delta_t * rate_row_ref[...]

    shard_log = nn(tri, pace, HIGHEST)
    last = shard_log[length - 1 : length, :]
    shard_grow = split(jnp.exp(shard_log), 3)
    shard_keep = split(jnp.exp(last - shard_log) * delta_t, 2)
    b_t = b_t_ref[...].astype(BF16)
    c_t = c_t_ref[...].astype(BF16)

    @pl.loop(0, pairs)
    def _(i):
        lanes = pl.ds(pl.multiple_of(i * LANES, LANES), LANES)
        chosen = head_lanes(heads, LANES, i * per)
        grow_x = spread_out(shard_grow, chosen)
        keep_x = spread_out(shard_keep, chosen)
        own_f[:, lanes] = nn(b_t, (x_ref[:, lanes].astype(F32) * keep_x).astype(BF16))
        own_b[:, lanes] = nn(c_t, (g_ref[:, lanes].astype(F32) * grow_x).astype(BF16))
        through_ref[:, lanes] = jnp.broadcast_to(grow_x[length - 1 : length, :], (8, LANES))

    rows = own_f.shape[0] // pieces

    def hop(source, landing, send, recv, k, target):
        part = pl.ds(pl.multiple_of(k * rows, rows), rows)
        return pltpu.make_async_remote_copy(
            src_ref=source.at[part],
            dst_ref=landing.at[part],
            send_sem=send.at[k],
            recv_sem=recv.at[k],
            device_id=(target, side),
            device_id_type=MESH,
        )

    def handle(k, place, own, landing, outgoing, send, recv, target):
        part = pl.ds(pl.multiple_of(k * rows, rows), rows)

        @pl.when(place == 0)
        def _():
            landing[part] = jnp.zeros((rows, width), F32)
            outgoing[part] = own[part]

        @pl.when(place > 0)
        def _():
            hop(outgoing, landing, send, recv, k, target).wait_recv()
            outgoing[part] = through_ref[0:1, :] * landing[part] + own[part]

        @pl.when(place < n_ctx - 1)
        def _():
            hop(outgoing, landing, send, recv, k, target).start()

    back = n_ctx - 1 - me

    def chain_lap(step):
        k_f, k_b = step - me, step - back

        @pl.when((k_f >= 0) & (k_f < pieces))
        def _():
            handle(k_f, me, own_f, in_f, out_f, send_f, recv_f, right)

        @pl.when((k_b >= 0) & (k_b < pieces))
        def _():
            handle(k_b, back, own_b, in_b, out_b, send_b, recv_b, left)

    chain_lap(0)

    log_rows = nn(delta * rate_col_ref[...], upper, HIGHEST)
    for h in range(heads):
        log_row[h] = log_rows[h : h + 1, :]
    log_t = nn(lower, pace, HIGHEST)
    ends = jnp.concatenate(
        [
            jnp.broadcast_to(log_t[(c + 1) * CHUNK - 1 : (c + 1) * CHUNK, :], (CHUNK, heads))
            for c in range(chunks)
        ],
        axis=0,
    )
    grow_hi[...], grow_lo[...] = split(jnp.exp(log_t), 2)
    keep_hi[...], keep_lo[...] = split(jnp.exp(ends - log_t) * delta_t, 2)
    off_hi[...], off_mid[...], off_lo[...] = split(jnp.log(delta_t) - log_t, 3)
    for c in range(chunks):
        part = slice(c * CHUNK, (c + 1) * CHUNK)
        gram_t[part] = nt(b_ref[part], c_ref[part], HIGHEST)
    dgram_t[...] = jnp.zeros_like(dgram_t)
    row_u[...] = jnp.zeros_like(row_u)
    row_v[...] = jnp.zeros_like(row_v)
    causal = iota((CHUNK, CHUNK), 1) >= iota((CHUNK, CHUNK), 0)
    first_half = iota((CHUNK, LANES), 1) < HEAD_DIM
    last_row = iota((CHUNK, LANES), 0) == CHUNK - 1
    head_id = iota((heads, CHUNK), 0)
    parts = [slice(c * CHUNK, (c + 1) * CHUNK) for c in range(chunks)]

    def within_unit(i):
        lanes = pl.ds(pl.multiple_of(i * LANES, LANES), LANES)
        offset = [off_hi[...], off_mid[...], off_lo[...]]
        columns = [
            spread_out(offset, (iota((heads, LANES), 0) == i * per + j).astype(BF16))
            for j in range(per)
        ]
        for part in parts:
            x_part, g_part = x_ref[part, lanes], g_ref[part, lanes]
            gram = gram_t[part]
            total = None
            within = []
            for j in range(per):
                mask = first_half if j == 0 else jnp.logical_not(first_half)
                x_half = jnp.where(mask, x_part.astype(F32), 0.0).astype(BF16)
                pair = nt(x_half, g_part)
                log_t_row = log_row[i * per + j, :, part]
                weight = jnp.exp(jnp.where(causal, log_t_row + columns[j][part], -1e30))
                value = weight * pair
                total = value if total is None else total + value
                summed = jnp.sum(value * gram, axis=0, keepdims=True)
                row_u[:, part] += jnp.where(head_id == i * per + j, summed, 0.0)
                within.append(nn((weight * gram).astype(BF16), g_part))
            dgram_t[part] += total
            inside[part, lanes] = jnp.where(first_half, within[0], within[1])

    capacity = act_ref.shape[1]
    before = (row_id < col_id).astype(BF16)

    def expert_unit(e, k):
        named = ids_ref[...] == side * experts + e
        hit = jnp.sum(named.astype(F32), axis=0, keepdims=True)
        rank = nn(jnp.broadcast_to(hit, (16, length)).astype(BF16), before)[0:1, :]
        place = jnp.where(hit > 0.5, rank, -1.0)
        picks = iota((capacity, length), 0).astype(F32) == place
        chosen = picks.astype(BF16)
        owner = lax.rem(side + n_exp - k, n_exp)
        columns = pl.ds(pl.multiple_of(owner * width, width), width)

        def product(grad):
            picked = nn(chosen, grad).astype(BF16)
            return nt(picked, w_ref[e, :, columns])

        @pl.when(k == 0)
        def _():
            act_sum[...] = product(g_ref[...])

        @pl.when(k > 0)
        def _():
            act_sum[...] += product(g_in[lax.max(k - 1, 0)])

        @pl.when(k == n_exp - 1)
        def _():
            prob = jnp.sum(jnp.where(named, probs_ref[...], 0.0), axis=0, keepdims=True)
            weight = jnp.sum(jnp.where(picks, prob, 0.0), axis=1, keepdims=True)
            inner = act_sum[...]
            grad_act_ref[e] = (weight * inner).astype(BF16)
            scored = act_ref[e].astype(F32) * inner
            ones = jnp.ones((16, scored.shape[1]), BF16)
            summed = None
            for piece in split(scored, 2):
                term = nt(ones, piece)
                summed = term if summed is None else summed + term
            grad_slots_ref[e] = summed[0:1, :]

    units = experts * n_exp
    laps = max(n_ctx - 1 + pieces, pairs + 1 + units)

    def lap(step, carry):
        chain_lap(step)

        @pl.when(step <= pairs)
        def _():
            within_unit(step - 1)

        @pl.when(step == pairs)
        def _():
            for e in range(experts):
                weights(e).wait()
            for k in range(1, n_exp):
                to_partner(k).wait_send()
            for k in range(1, n_exp):
                to_partner(k).wait_recv()

        unit = step - pairs - 1

        @pl.when((unit >= 0) & (unit < units))
        def _():
            expert_unit(unit // n_exp, lax.rem(unit, n_exp))

        return carry

    lax.fori_loop(1, laps, lap, 0)

    @pl.when(me < n_ctx - 1)
    def _():
        for k in range(pieces):
            hop(out_f, in_f, send_f, recv_f, k, right).wait_send()

    @pl.when(back < n_ctx - 1)
    def _():
        for k in range(pieces):
            hop(out_b, in_b, send_b, recv_b, k, left).wait_send()

    for part in parts:
        part_b[part] = nn(dgram_t[part], c_ref[part], HIGHEST)
        part_c[part] = nn(dgram_t[part].T, b_ref[part], HIGHEST)

    @pl.loop(0, pairs)
    def _(i):
        lanes = pl.ds(pl.multiple_of(i * LANES, LANES), LANES)
        chosen = head_lanes(heads, LANES, i * per)
        grow_x = spread_out([grow_hi[...], grow_lo[...]], chosen)
        keep_x = spread_out([keep_hi[...], keep_lo[...]], chosen)
        skip = skip_ref[0:1, lanes]
        xs = [x_ref[part, lanes].astype(F32) for part in parts]
        gs = [g_ref[part, lanes].astype(F32) for part in parts]
        kept = [(xs[c] * keep_x[parts[c]]).astype(BF16) for c in range(chunks)]
        grown = [(gs[c] * grow_x[parts[c]]).astype(BF16) for c in range(chunks)]
        through = [grow_x[(c + 1) * CHUNK - 1 : (c + 1) * CHUNK, :] for c in range(chunks)]
        states = [in_f[:, lanes]]
        for c in range(chunks):
            states.append(
                through[c] * states[c] + nn(b_t_ref[:, parts[c]].astype(BF16), kept[c])
            )
        grads = [None] * chunks + [in_b[:, lanes]]
        for c in reversed(range(chunks)):
            grads[c] = through[c] * grads[c + 1] + nn(c_t_ref[:, parts[c]].astype(BF16), grown[c])
        for c in range(chunks):
            part = parts[c]
            state, grad = states[c].astype(BF16), grads[c + 1].astype(BF16)
            from_grad = nn(b_ref[part].astype(BF16), grad) * keep_x[part]
            from_state = nn(c_ref[part].astype(BF16), state) * grow_x[part]
            part_c[part] += nt(grown[c], state)
            part_b[part] += nt(kept[c], grad)
            inner = inside[part, lanes] + from_grad
            grad_x_ref[part, lanes] = (inner + skip * gs[c]).astype(BF16)
            used = xs[c] * inner
            ending = jnp.sum(states[c + 1] * grads[c + 1], axis=0, keepdims=True)
            reached = gs[c] * from_state + jnp.where(last_row, ending, 0.0)
            for piece in split(used, 2):
                row_v[:, part] += nt(chosen, piece)
            for piece in split(reached, 2):
                row_u[:, part] += nt(chosen, piece)

    share = grad_b_ref.shape[0]

    def shed(k, source, landing, send, recv):
        target = lax.rem(side + k, n_exp)
        return pltpu.make_async_remote_copy(
            src_ref=source.at[pl.ds(pl.multiple_of(target * share, share), share)],
            dst_ref=landing.at[k - 1],
            send_sem=send.at[k - 1],
            recv_sem=recv.at[k - 1],
            device_id=(me, target),
            device_id_type=MESH,
        )

    for k in range(1, n_exp):
        shed(k, part_b, land_b, send_p, recv_p).start()
        shed(k, part_c, land_c, send_q, recv_q).start()
    drift = nn(row_u[...] - row_v[...], lower, HIGHEST)
    grad_delta_ref[...] = row_v[...] / delta + rate_col_ref[...] * drift
    mine = pl.ds(pl.multiple_of(side * share, share), share)
    total_b, total_c = part_b[mine], part_c[mine]
    for k in range(1, n_exp):
        shed(k, part_b, land_b, send_p, recv_p).wait()
        shed(k, part_c, land_c, send_q, recv_q).wait()
        total_b = total_b + land_b[k - 1]
        total_c = total_c + land_c[k - 1]
    grad_b_ref[...] = total_b
    grad_c_ref[...] = total_c


def per_device(
    n_ctx, n_exp,
    feature_in, grad_out, delta, decay_log, skip_gain, b_proj, c_proj,
    route_ids, route_probs, w_down, saved_act,
):
    length, width = feature_in.shape
    heads = delta.shape[0]
    nstate = b_proj.shape[1]
    experts, hidden, full = w_down.shape
    capacity = saved_act.shape[2]
    share = length // n_exp
    others = n_exp - 1
    rate = -jnp.exp(decay_log)
    rate_row, rate_col = rate[None, :], rate[:, None]
    skip = jnp.repeat(skip_gain, HEAD_DIM)[None, :]
    vmem = pl.BlockSpec(memory_space=pltpu.VMEM)
    hbm = pl.BlockSpec(memory_space=pl.ANY)
    pieces = nstate // 8
    dma = pltpu.SemaphoreType.DMA
    shard = jax.ShapeDtypeStruct((share, nstate), F32)
    square = pltpu.VMEM((length, nstate), F32)
    by_head = pltpu.VMEM((heads, length), F32)
    grad_x, grad_delta, grad_b, grad_c, grad_act, grad_slots = pl.pallas_call(
        partial(block_kernel, n_ctx, n_exp, pieces),
        out_shape=(
            jax.ShapeDtypeStruct((length, width), BF16),
            jax.ShapeDtypeStruct((heads, length), F32),
            shard,
            shard,
            jax.ShapeDtypeStruct((experts, capacity, hidden), BF16),
            jax.ShapeDtypeStruct((experts, 1, capacity), F32),
        ),
        in_specs=[vmem] * 14 + [hbm],
        out_specs=(vmem,) * 6,
        scratch_shapes=[pltpu.VMEM((nstate, width), F32)] * 6
        + [pltpu.VMEM((8, width), F32)]
        + [pltpu.VMEM((others, length, width), BF16)]
        + [pltpu.VMEM((experts, hidden, full), BF16)]
        + [pltpu.VMEM((heads, 1, length), F32)]
        + [pltpu.VMEM((length, heads), BF16)] * 7
        + [pltpu.VMEM((length, CHUNK), F32)] * 2
        + [by_head] * 2
        + [pltpu.VMEM((length, width), F32)]
        + [square] * 2
        + [pltpu.VMEM((others, share, nstate), F32)] * 2
        + [pltpu.VMEM((capacity, hidden), F32)]
        + [dma((pieces,))] * 4
        + [dma((others,))] * 2
        + [dma((experts,))]
        + [dma((others,))] * 4,
        compiler_params=pltpu.CompilerParams(
            collective_id=0, has_side_effects=True, vmem_limit_bytes=50 << 20
        ),
        name="block_grads",
    )(
        feature_in, grad_out, delta, delta.T, rate_row, rate_col, skip,
        b_proj, c_proj, b_proj.T, c_proj.T, route_ids.T, route_probs.T, saved_act[0], w_down,
    )
    return (grad_x, grad_delta, grad_b, grad_c, grad_act[None], grad_slots.reshape(1, experts, capacity))


def solution(mesh):
    placed = (
        P("ctx", "exp"),
        P("ctx", "exp"),
        P("exp", "ctx"),
        P("exp"),
        P("exp"),
        P("ctx", None),
        P("ctx", None),
        P("ctx", None),
        P("ctx", None),
        P("exp", None, None),
        P("ctx", "exp", None, None),
    )
    return jax.shard_map(
        partial(per_device, mesh.shape["ctx"], mesh.shape["exp"]),
        mesh=mesh,
        in_specs=placed,
        out_specs=(
            P("ctx", "exp"),
            P("exp", "ctx"),
            P(("ctx", "exp"), None),
            P(("ctx", "exp"), None),
            P("ctx", "exp", None, None),
            P("ctx", "exp", None),
        ),
        check_vma=False,
    )
```

```python
from functools import partial

import jax
import jax.numpy as jnp
from jax import lax
from jax.experimental import pallas as pl
from jax.experimental.pallas import tpu as pltpu
from jax.sharding import PartitionSpec as P

HEAD_DIM = 64
CHUNK = 128
LANES = 128
HOP_LAPS = 2
HIGHEST = lax.Precision.HIGHEST
F32 = jnp.float32
BF16 = jnp.bfloat16
MESH = pl.DeviceIdType.MESH


def nn(a, b, precision=None):
    return lax.dot_general(
        a, b, (((1,), (0,)), ((), ())), precision=precision, preferred_element_type=F32
    )


def nt(a, b, precision=None):
    return lax.dot_general(
        a, b, (((1,), (1,)), ((), ())), precision=precision, preferred_element_type=F32
    )


def split(value, count):
    parts = []
    for _ in range(count):
        part = value.astype(BF16)
        parts.append(part)
        value = value - part.astype(F32)
    return parts


def spread_out(parts, chosen):
    total = nn(parts[0], chosen)
    for part in parts[1:]:
        total = total + nn(part, chosen)
    return total


def iota(shape, dim):
    return lax.broadcasted_iota(jnp.int32, shape, dim)


def head_lanes(heads, width, first):
    return (iota((heads, width), 0) == first + iota((heads, width), 1) // HEAD_DIM).astype(BF16)


def block_kernel(
    n_ctx, n_exp, pieces,
    x_ref, g_ref, delta_ref, delta_t_ref, rate_row_ref, rate_col_ref, skip_ref,
    b_ref, c_ref, ids_ref, probs_ref, act_ref, w_any,
    grad_x_ref, grad_delta_ref, grad_b_ref, grad_c_ref, grad_act_ref, grad_slots_ref,
    own_f, own_b, in_f, in_b, out_f, out_b, through_ref, g_in, w_ref,
    log_row, grow_hi, grow_lo, keep_hi, keep_lo, off_hi, off_mid, off_lo,
    gram_t, dgram_t, row_u, row_v, inside, part_b, part_c, land_b, land_c, act_sum, b_t_ref, c_t_ref,
    send_f, recv_f, send_b, recv_b, send_g, recv_g, load_w, send_p, recv_p, send_q, recv_q,
):
    me, side = lax.axis_index("ctx"), lax.axis_index("exp")
    right, left = lax.rem(me + 1, n_ctx), lax.rem(me + n_ctx - 1, n_ctx)
    barrier = pltpu.get_barrier_semaphore()
    for other in (left, right):
        pl.semaphore_signal(barrier, inc=1, device_id=(other, side), device_id_type=MESH)
    for k in range(1, n_exp):
        pl.semaphore_signal(
            barrier, inc=1, device_id=(me, lax.rem(side + k, n_exp)), device_id_type=MESH
        )
    pl.semaphore_wait(barrier, 2 + n_exp - 1)

    def to_partner(k):
        return pltpu.make_async_remote_copy(
            src_ref=g_ref,
            dst_ref=g_in.at[k - 1],
            send_sem=send_g.at[k - 1],
            recv_sem=recv_g.at[k - 1],
            device_id=(me, lax.rem(side + k, n_exp)),
            device_id_type=MESH,
        )

    for k in range(1, n_exp):
        to_partner(k).start()
    experts = w_ref.shape[0]

    def weights(e):
        return pltpu.make_async_copy(w_any.at[e], w_ref.at[e], load_w.at[e])

    for e in range(experts):
        weights(e).start()

    length, width = x_ref.shape
    heads = delta_t_ref.shape[1]
    chunks = length // CHUNK
    per = LANES // HEAD_DIM
    pairs = width // LANES
    delta, delta_t = delta_ref[...], delta_t_ref[...]
    row_id, col_id = iota((length, length), 0), iota((length, length), 1)
    same = row_id // CHUNK == col_id // CHUNK
    tri = (row_id >= col_id).astype(F32)
    lower = ((row_id >= col_id) & same).astype(F32)
    upper = ((row_id <= col_id) & same).astype(F32)
    pace = delta_t * rate_row_ref[...]

    shard_log = nn(tri, pace, HIGHEST)
    last = shard_log[length - 1 : length, :]
    shard_grow = split(jnp.exp(shard_log), 2)
    shard_keep = split(jnp.exp(last - shard_log) * delta_t, 2)
    b_t = b_ref[...].T.astype(BF16)
    c_t = c_ref[...].T.astype(BF16)
    b_t_ref[...] = b_t
    c_t_ref[...] = c_t

    @pl.loop(0, pairs)
    def _(i):
        lanes = pl.ds(pl.multiple_of(i * LANES, LANES), LANES)
        chosen = head_lanes(heads, LANES, i * per)
        grow_x = spread_out(shard_grow, chosen)
        keep_x = spread_out(shard_keep, chosen)
        own_f[:, lanes] = nn(b_t, (x_ref[:, lanes].astype(F32) * keep_x).astype(BF16))
        own_b[:, lanes] = nn(c_t, (g_ref[:, lanes].astype(F32) * grow_x).astype(BF16))
        through_ref[:, lanes] = jnp.broadcast_to(grow_x[length - 1 : length, :], (8, LANES))

    rows = own_f.shape[0] // pieces

    def hop(source, landing, send, recv, k, target):
        part = pl.ds(pl.multiple_of(k * rows, rows), rows)
        return pltpu.make_async_remote_copy(
            src_ref=source.at[part],
            dst_ref=landing.at[part],
            send_sem=send.at[k],
            recv_sem=recv.at[k],
            device_id=(target, side),
            device_id_type=MESH,
        )

    def handle(k, place, own, landing, outgoing, send, recv, target):
        part = pl.ds(pl.multiple_of(k * rows, rows), rows)

        @pl.when(place == 0)
        def _():
            landing[part] = jnp.zeros((rows, width), F32)
            outgoing[part] = own[part]

        @pl.when(place > 0)
        def _():
            hop(outgoing, landing, send, recv, k, target).wait_recv()
            outgoing[part] = through_ref[0:1, :] * landing[part] + own[part]

        @pl.when(place < n_ctx - 1)
        def _():
            hop(outgoing, landing, send, recv, k, target).start()

    back = n_ctx - 1 - me

    def first_lap(place):
        return (place + 1) // 2 + HOP_LAPS * (place // 2)

    start_f, start_b = first_lap(me), first_lap(back)

    def chain_lap(step):
        k_f, k_b = step - start_f, step - start_b

        @pl.when((k_f >= 0) & (k_f < pieces))
        def _():
            handle(k_f, me, own_f, in_f, out_f, send_f, recv_f, right)

        @pl.when((k_b >= 0) & (k_b < pieces))
        def _():
            handle(k_b, back, own_b, in_b, out_b, send_b, recv_b, left)

    chain_lap(0)

    log_rows = nn(delta * rate_col_ref[...], upper, HIGHEST)
    for h in range(heads):
        log_row[h] = log_rows[h : h + 1, :]
    log_t = nn(lower, pace, HIGHEST)
    ends = jnp.concatenate(
        [
            jnp.broadcast_to(log_t[(c + 1) * CHUNK - 1 : (c + 1) * CHUNK, :], (CHUNK, heads))
            for c in range(chunks)
        ],
        axis=0,
    )
    grow_hi[...], grow_lo[...] = split(jnp.exp(log_t), 2)
    keep_hi[...], keep_lo[...] = split(jnp.exp(ends - log_t) * delta_t, 2)
    off_hi[...], off_mid[...], off_lo[...] = split(jnp.log(delta_t) - log_t, 3)
    for c in range(chunks):
        part = slice(c * CHUNK, (c + 1) * CHUNK)
        gram_t[part] = nt(b_ref[part], c_ref[part], HIGHEST)
    dgram_t[...] = jnp.zeros_like(dgram_t)
    row_u[...] = jnp.zeros_like(row_u)
    row_v[...] = jnp.zeros_like(row_v)
    causal = iota((CHUNK, CHUNK), 1) >= iota((CHUNK, CHUNK), 0)
    first_half = iota((CHUNK, LANES), 1) < HEAD_DIM
    last_row = iota((CHUNK, LANES), 0) == CHUNK - 1
    head_id = iota((heads, CHUNK), 0)
    parts = [slice(c * CHUNK, (c + 1) * CHUNK) for c in range(chunks)]

    def within_unit(i):
        lanes = pl.ds(pl.multiple_of(i * LANES, LANES), LANES)
        offset = [off_hi[...], off_mid[...], off_lo[...]]
        columns = [
            spread_out(offset, (iota((heads, LANES), 0) == i * per + j).astype(BF16))
            for j in range(per)
        ]
        for part in parts:
            x_part, g_part = x_ref[part, lanes], g_ref[part, lanes]
            gram = gram_t[part]
            total = None
            within = []
            for j in range(per):
                mask = first_half if j == 0 else jnp.logical_not(first_half)
                x_half = jnp.where(mask, x_part.astype(F32), 0.0).astype(BF16)
                pair = nt(x_half, g_part)
                log_t_row = log_row[i * per + j, :, part]
                weight = jnp.exp(jnp.where(causal, log_t_row + columns[j][part], -1e30))
                value = weight * pair
                total = value if total is None else total + value
                summed = jnp.sum(value * gram, axis=0, keepdims=True)
                row_u[:, part] += jnp.where(head_id == i * per + j, summed, 0.0)
                within.append(nn((weight * gram).astype(BF16), g_part))
            dgram_t[part] += total
            inside[part, lanes] = jnp.where(first_half, within[0], within[1])

    capacity = act_ref.shape[1]
    before = (row_id < col_id).astype(BF16)

    def expert_unit(e, k):
        named = ids_ref[...] == side * experts + e
        hit = jnp.sum(named.astype(F32), axis=0, keepdims=True)
        rank = nn(jnp.broadcast_to(hit, (16, length)).astype(BF16), before)[0:1, :]
        place = jnp.where(hit > 0.5, rank, -1.0)
        picks = iota((capacity, length), 0).astype(F32) == place
        chosen = picks.astype(BF16)
        owner = lax.rem(side + n_exp - k, n_exp)
        columns = pl.ds(pl.multiple_of(owner * width, width), width)

        def product(grad):
            picked = nn(chosen, grad).astype(BF16)
            return nt(picked, w_ref[e, :, columns])

        @pl.when(k == 0)
        def _():
            act_sum[...] = product(g_ref[...])

        @pl.when(k > 0)
        def _():
            act_sum[...] += product(g_in[lax.max(k - 1, 0)])

        @pl.when(k == n_exp - 1)
        def _():
            prob = jnp.sum(jnp.where(named, probs_ref[...], 0.0), axis=0, keepdims=True)
            weight = jnp.sum(jnp.where(picks, prob, 0.0), axis=1, keepdims=True)
            inner = act_sum[...]
            grad_act_ref[e] = (weight * inner).astype(BF16)
            scored = act_ref[e].astype(F32) * inner
            ones = jnp.ones((16, scored.shape[1]), BF16)
            summed = None
            for piece in split(scored, 2):
                term = nt(ones, piece)
                summed = term if summed is None else summed + term
            grad_slots_ref[e] = summed[0:1, :]

    units = experts * n_exp
    laps = max(first_lap(n_ctx - 1) + pieces, pairs + 1 + units)

    def lap(step, carry):
        chain_lap(step)

        @pl.when(step <= pairs)
        def _():
            within_unit(step - 1)

        @pl.when(step == pairs)
        def _():
            for e in range(experts):
                weights(e).wait()
            for k in range(1, n_exp):
                to_partner(k).wait_send()
            for k in range(1, n_exp):
                to_partner(k).wait_recv()

        unit = step - pairs - 1

        @pl.when((unit >= 0) & (unit < units))
        def _():
            expert_unit(unit // n_exp, lax.rem(unit, n_exp))

        return carry

    lax.fori_loop(1, laps, lap, 0)

    @pl.when(me < n_ctx - 1)
    def _():
        for k in range(pieces):
            hop(out_f, in_f, send_f, recv_f, k, right).wait_send()

    @pl.when(back < n_ctx - 1)
    def _():
        for k in range(pieces):
            hop(out_b, in_b, send_b, recv_b, k, left).wait_send()

    for part in parts:
        part_b[part] = nn(dgram_t[part], c_ref[part], HIGHEST)
        part_c[part] = nn(dgram_t[part].T, b_ref[part], HIGHEST)

    @pl.loop(0, pairs)
    def _(i):
        lanes = pl.ds(pl.multiple_of(i * LANES, LANES), LANES)
        chosen = head_lanes(heads, LANES, i * per)
        grow_x = spread_out([grow_hi[...], grow_lo[...]], chosen)
        keep_x = spread_out([keep_hi[...], keep_lo[...]], chosen)
        skip = skip_ref[0:1, lanes]
        xs = [x_ref[part, lanes].astype(F32) for part in parts]
        gs = [g_ref[part, lanes].astype(F32) for part in parts]
        kept = [(xs[c] * keep_x[parts[c]]).astype(BF16) for c in range(chunks)]
        grown = [(gs[c] * grow_x[parts[c]]).astype(BF16) for c in range(chunks)]
        through = [grow_x[(c + 1) * CHUNK - 1 : (c + 1) * CHUNK, :] for c in range(chunks)]
        states = [in_f[:, lanes]]
        for c in range(chunks):
            states.append(
                through[c] * states[c] + nn(b_t_ref[:, parts[c]], kept[c])
            )
        grads = [None] * chunks + [in_b[:, lanes]]
        for c in reversed(range(chunks)):
            grads[c] = through[c] * grads[c + 1] + nn(c_t_ref[:, parts[c]], grown[c])
        for c in range(chunks):
            part = parts[c]
            state, grad = states[c].astype(BF16), grads[c + 1].astype(BF16)
            from_grad = nn(b_ref[part].astype(BF16), grad) * keep_x[part]
            from_state = nn(c_ref[part].astype(BF16), state) * grow_x[part]
            part_c[part] += nt(grown[c], state)
            part_b[part] += nt(kept[c], grad)
            inner = inside[part, lanes] + from_grad
            grad_x_ref[part, lanes] = (inner + skip * gs[c]).astype(BF16)
            used = xs[c] * inner
            ending = jnp.sum(states[c + 1] * grads[c + 1], axis=0, keepdims=True)
            reached = gs[c] * from_state + jnp.where(last_row, ending, 0.0)
            for piece in split(used, 2):
                row_v[:, part] += nt(chosen, piece)
            for piece in split(reached, 2):
                row_u[:, part] += nt(chosen, piece)

    share = grad_b_ref.shape[0]

    def shed(k, source, landing, send, recv):
        target = lax.rem(side + k, n_exp)
        return pltpu.make_async_remote_copy(
            src_ref=source.at[pl.ds(pl.multiple_of(target * share, share), share)],
            dst_ref=landing.at[k - 1],
            send_sem=send.at[k - 1],
            recv_sem=recv.at[k - 1],
            device_id=(me, target),
            device_id_type=MESH,
        )

    for k in range(1, n_exp):
        shed(k, part_b, land_b, send_p, recv_p).start()
        shed(k, part_c, land_c, send_q, recv_q).start()
    drift = nn(row_u[...] - row_v[...], lower, HIGHEST)
    grad_delta_ref[...] = row_v[...] / delta + rate_col_ref[...] * drift
    mine = pl.ds(pl.multiple_of(side * share, share), share)
    total_b, total_c = part_b[mine], part_c[mine]
    for k in range(1, n_exp):
        shed(k, part_b, land_b, send_p, recv_p).wait()
        shed(k, part_c, land_c, send_q, recv_q).wait()
        total_b = total_b + land_b[k - 1]
        total_c = total_c + land_c[k - 1]
    grad_b_ref[...] = total_b
    grad_c_ref[...] = total_c


def per_device(
    n_ctx, n_exp,
    feature_in, grad_out, delta, decay_log, skip_gain, b_proj, c_proj,
    route_ids, route_probs, w_down, saved_act,
):
    length, width = feature_in.shape
    heads = delta.shape[0]
    nstate = b_proj.shape[1]
    experts, hidden, full = w_down.shape
    capacity = saved_act.shape[2]
    share = length // n_exp
    others = n_exp - 1
    rate = -jnp.exp(decay_log)
    rate_row, rate_col = rate[None, :], rate[:, None]
    skip = jnp.repeat(skip_gain, HEAD_DIM)[None, :]
    vmem = pl.BlockSpec(memory_space=pltpu.VMEM)
    hbm = pl.BlockSpec(memory_space=pl.ANY)
    pieces = nstate // 16
    dma = pltpu.SemaphoreType.DMA
    shard = jax.ShapeDtypeStruct((share, nstate), F32)
    square = pltpu.VMEM((length, nstate), F32)
    by_head = pltpu.VMEM((heads, length), F32)
    grad_x, grad_delta, grad_b, grad_c, grad_act, grad_slots = pl.pallas_call(
        partial(block_kernel, n_ctx, n_exp, pieces),
        out_shape=(
            jax.ShapeDtypeStruct((length, width), BF16),
            jax.ShapeDtypeStruct((heads, length), F32),
            shard,
            shard,
            jax.ShapeDtypeStruct((experts, capacity, hidden), BF16),
            jax.ShapeDtypeStruct((experts, 1, capacity), F32),
        ),
        in_specs=[vmem] * 12 + [hbm],
        out_specs=(vmem,) * 6,
        scratch_shapes=[pltpu.VMEM((nstate, width), F32)] * 6
        + [pltpu.VMEM((8, width), F32)]
        + [pltpu.VMEM((others, length, width), BF16)]
        + [pltpu.VMEM((experts, hidden, full), BF16)]
        + [pltpu.VMEM((heads, 1, length), F32)]
        + [pltpu.VMEM((length, heads), BF16)] * 7
        + [pltpu.VMEM((length, CHUNK), F32)] * 2
        + [by_head] * 2
        + [pltpu.VMEM((length, width), F32)]
        + [square] * 2
        + [pltpu.VMEM((others, share, nstate), F32)] * 2
        + [pltpu.VMEM((capacity, hidden), F32)]
        + [pltpu.VMEM((nstate, length), BF16)] * 2
        + [dma((pieces,))] * 4
        + [dma((others,))] * 2
        + [dma((experts,))]
        + [dma((others,))] * 4,
        compiler_params=pltpu.CompilerParams(
            collective_id=0, has_side_effects=True, vmem_limit_bytes=50 << 20
        ),
        name="block_grads",
    )(
        feature_in, grad_out, delta, delta.T, rate_row, rate_col, skip,
        b_proj, c_proj, route_ids.T, route_probs.T, saved_act[0], w_down,
    )
    return (grad_x, grad_delta, grad_b, grad_c, grad_act[None], grad_slots.reshape(1, experts, capacity))


def solution(mesh):
    placed = (
        P("ctx", "exp"),
        P("ctx", "exp"),
        P("exp", "ctx"),
        P("exp"),
        P("exp"),
        P("ctx", None),
        P("ctx", None),
        P("ctx", None),
        P("ctx", None),
        P("exp", None, None),
        P("ctx", "exp", None, None),
    )
    return jax.shard_map(
        partial(per_device, mesh.shape["ctx"], mesh.shape["exp"]),
        mesh=mesh,
        in_specs=placed,
        out_specs=(
            P("ctx", "exp"),
            P("exp", "ctx"),
            P(("ctx", "exp"), None),
            P(("ctx", "exp"), None),
            P("ctx", "exp", None, None),
            P("ctx", "exp", None),
        ),
        check_vma=False,
    )
```
